256 devices in a mesh: row: 16 (over z, core), col: 16 (over y, x).
Axes of the slice: x: 4, y: 4, z: 8, core: 2. Of those that a mesh axis runs over, the one named last changes fastest.
Arguments:
- tokens: bfloat16 [2048, 6144], P('col', 'row'), may hold values from -6 to 6
- up_latent: bfloat16 [6144, 24576], P('row', 'col'), may hold values from -1.0206207 to 1.0206207
- down_latent: bfloat16 [24576, 6144], P('col', 'row'), may hold values from -0.51031036 to 0.51031036
- out_grad: bfloat16 [2048, 6144], P('col', 'row'), may hold values from -6 to 6
Outputs:
- output: bfloat16 [2048, 6144], P('col', 'row')
- in_grad: bfloat16 [2048, 6144], P('col', 'row')
- up_grad: bfloat16 [6144, 24576], P('row', 'col')
- down_grad: bfloat16 [24576, 6144], P('col', 'row')
The draws below stay inside these ranges and needn't reach their ends.
All inputs are finite; a program needn't handle non-finite values.
Results may differ from the reference program's by a relative error of at most 0.028.
Values may be sent and summed in bfloat16 or wider, within the bound.
No kernel may reach another device: no remote copies, remote signals or barrier semaphores. Data moves between devices by JAX's collectives and lax.ppermute only.
A program may use at most 128 MiB of HBM per device.

```python
import math
import jax
import jax.numpy as jnp
from jax import lax

D = 6144
FFW = 24576
TOKENS = 2048
N_ROW = 16
N_COL = 16


def latent_matrix(key, row_total, col_total, fan_in):
    key_rows, key_cols, key_base = jax.random.split(key, 3)
    trend = 3.0 ** (jnp.arange(row_total, dtype=jnp.float32) / max(row_total - 1, 1))
    row_scale = 10.0 ** (0.5 * jax.random.uniform(key_rows, (row_total, 1), jnp.float32)) * trend[:, None]
    col_scale = 10.0 ** (0.5 * jax.random.uniform(key_cols, (1, col_total), jnp.float32))
    base = jnp.clip(jax.random.normal(key_base, (row_total, col_total), jnp.float32), -4.0, 4.0)
    limit = 79.0 * fan_in ** (-0.5)
    values = jnp.clip(base * row_scale * col_scale * (0.5 * fan_in ** (-0.5)), -limit, limit)
    return values.astype(jnp.bfloat16)


def draw_up_latent(key, part):
    return latent_matrix(jax.random.fold_in(key, 11), D, FFW, D)


def draw_down_latent(key, part):
    return latent_matrix(jax.random.fold_in(key, 23), FFW, D, FFW)


def levels(own_key, extent, pieces, least, high):
    def one(axis_at, parts):
        draws = jax.random.uniform(jax.random.fold_in(jax.random.fold_in(own_key, 6), axis_at), (parts,), jnp.float32, least / len(pieces), high / len(pieces))
        return jnp.repeat(jnp.exp(draws), extent[axis_at] // parts).reshape((-1,) + (1,) * (len(extent) - axis_at - 1))

    loudness = one(*pieces[0])
    for cut in pieces[1:]:
        loudness = loudness * one(*cut)
    return loudness


def bell_draw(own_key, extent, deviation, bound, cuts=(), kind=jnp.bfloat16):
    level = levels(own_key, extent, cuts, -0.22, 0.18) if cuts else 1.0
    result = jax.random.normal(own_key, extent, jnp.float32) * deviation * level
    return jnp.minimum(jnp.maximum(result, -bound), bound).astype(kind)


def setup_inputs(seed: int = 0) -> dict:
    key_of = jax.random.split(jax.random.key(seed), 5)
    return {
        "tokens": bell_draw(key_of[0], (TOKENS, D), 1.0, 6.0, ((0, 16), (1, 16))),
        "up_latent": draw_up_latent(jax.random.fold_in(key_of[4], 71), 0),
        "down_latent": draw_down_latent(jax.random.fold_in(key_of[4], 71), 0),
        "out_grad": bell_draw(key_of[3], (TOKENS, D), 1.0, 6.0, ((0, 16), (1, 16))),
    }


gelu_coef = math.sqrt(2.0 / math.pi)

def gelu_value(values):
    tanh_arg = gelu_coef * (values + 0.044715 * values * values * values)
    return 0.5 * values * (1.0 + jnp.tanh(tanh_arg))

def gelu_slope(values):
    tanh_val = jnp.tanh(gelu_coef * (values + 0.044715 * values * values * values))
    return 0.5 * (1.0 + tanh_val) + 0.5 * values * (1.0 - tanh_val * tanh_val) * gelu_coef * (1.0 + 3.0 * 0.044715 * values * values)

def ternary(latent, fan_in):
    limit = 0.8 * fan_in ** (-0.5)
    wide = latent.astype(jnp.float32)
    upper = jnp.where(wide > limit, 1.0, 0.0)
    lower = jnp.where(wide < -limit, 1.0, 0.0)
    return (upper - lower).astype(jnp.bfloat16)

def rounded(values):
    return lax.optimization_barrier(values.astype(jnp.bfloat16)).astype(jnp.float32)

def blocked_sum(left, right, count, scale, transposed):
    width = left.shape[1] // count
    total = None
    for index in range(count):
        left_block = left[:, index * width:(index + 1) * width]
        if transposed:
            right_block = right[:, index * width:(index + 1) * width].T
        else:
            right_block = right[index * width:(index + 1) * width, :]
        partial_sum = scale * jnp.dot(left_block, right_block, preferred_element_type=jnp.float32)
        term = rounded(partial_sum)
        total = term if total is None else total + term
    return total

def reference(tokens, up_latent, down_latent, out_grad):
    up_scale = jnp.sum(jnp.abs(up_latent.astype(jnp.float32))) / (D * FFW)
    down_scale = jnp.sum(jnp.abs(down_latent.astype(jnp.float32))) / (D * FFW)
    up_tern = ternary(up_latent, D)
    down_tern = ternary(down_latent, FFW)
    grad_norm = 1.0 / math.sqrt(TOKENS)
    hidden = blocked_sum(tokens, up_tern, N_ROW, up_scale, False)
    act = gelu_value(hidden).astype(jnp.bfloat16)
    output = blocked_sum(act, down_tern, N_COL, down_scale, False).astype(jnp.bfloat16)
    down_grad = (jnp.dot(act.T, out_grad, preferred_element_type=jnp.float32) * grad_norm).astype(jnp.bfloat16)
    act_grad = blocked_sum(out_grad, down_tern, N_ROW, down_scale, True)
    hidden_grad = (act_grad * gelu_slope(hidden)).astype(jnp.bfloat16)
    up_grad = (jnp.dot(tokens.T, hidden_grad, preferred_element_type=jnp.float32) * grad_norm).astype(jnp.bfloat16)
    in_grad = blocked_sum(hidden_grad, up_tern, N_COL, up_scale, True).astype(jnp.bfloat16)
    return (output, in_grad, up_grad, down_grad)
```

```python
import math

import jax
import jax.numpy as jnp
from jax import lax
from jax.sharding import Mesh
from jax.sharding import PartitionSpec as P

Z, C, Y, X = "row_0", "row_1", "col_0", "col_1"
ROW = (Z, C)
COL = (Y, X)
F32 = jnp.float32
BF16 = jnp.bfloat16


gelu_coef = math.sqrt(2.0 / math.pi)


def shifted(value, axis, step):
    count = lax.axis_size(axis)
    return lax.ppermute(value, axis, [(i, (i + step) % count) for i in range(count)])


def swapped(value):
    return lax.ppermute(value, C, [(0, 1), (1, 0)])


def ternary(latent, fan_in):
    limit = 0.8 * fan_in ** (-0.5)
    wide = latent.astype(F32)
    return jnp.where(wide > limit, 1.0, jnp.where(wide < -limit, -1.0, 0.0)).astype(BF16)


def dot(left, right, left_dim, right_dim):
    return lax.dot_general(
        left, right, (((left_dim,), (right_dim,)), ((), ())), preferred_element_type=F32
    )


def ring_pieces(value, axis):
    count = lax.axis_size(axis)
    return [value] + [shifted(value, axis, -d) for d in range(1, count)]


def gathered(value, first, second):
    inner = jnp.stack(ring_pieces(value, first))
    return ring_pieces(inner, second)


def sent_home(pieces, axis):
    total = pieces[0].astype(F32)
    for d in range(1, len(pieces)):
        total = total + shifted(pieces[d], axis, d).astype(F32)
    return total


def body(tokens, up_latent, down_latent, out_grad):
    depth = lax.axis_size(Z)
    cols_axis = lax.axis_size(COL)
    rows_axis = lax.axis_size(ROW)
    core = lax.axis_index(C)
    fan_up = up_latent.shape[0] * rows_axis
    fan_down = down_latent.shape[0] * cols_axis
    entry_total = fan_up * fan_down
    width = tokens.shape[1]
    block = tokens.shape[0]
    half = block // 2
    token_total = block * cols_axis
    grad_norm = 1.0 / math.sqrt(token_total)

    pair = jnp.stack([tokens, out_grad])
    mine = lax.dynamic_slice_in_dim(pair, core * half, half, axis=1)
    theirs = lax.dynamic_slice_in_dim(pair, (1 - core) * half, half, axis=1)
    pair = jnp.concatenate([mine, swapped(theirs)], axis=2)
    up_other = swapped(up_latent)
    down_other = swapped(down_latent)

    tok = gathered(pair[0], X, Y)
    grd = gathered(pair[1], Y, X)
    tok_all = jnp.stack(tok, axis=0).reshape(-1, 2 * width)
    grd_all = jnp.stack(grd, axis=1).reshape(-1, 2 * width)

    up_tern = jnp.concatenate([ternary(up_latent, fan_up), ternary(up_other, fan_up)], axis=0)
    down_tern = jnp.concatenate(
        [ternary(down_latent, fan_down), ternary(down_other, fan_down)], axis=1
    )
    hidden_width = up_tern.shape[1]

    hid_part = dot(tok_all, up_tern, 1, 0).astype(BF16).reshape(depth, -1, hidden_width)
    hid_sum = lax.psum_scatter(hid_part, Z, scatter_dimension=0, tiled=False)
    act_part = dot(grd_all, down_tern, 1, 1).astype(BF16).reshape(depth, -1, hidden_width)
    act_parts = lax.all_to_all(act_part, Z, 0, 0, tiled=True)

    sums = (
        jnp.sum(jnp.abs(up_latent.astype(F32))),
        jnp.sum(jnp.abs(down_latent.astype(F32))),
    )
    sums = lax.optimization_barrier((*sums, act_part))[:2]
    for axis in (C, Z, Y, X):
        sums = lax.psum(sums, axis)
    up_scale = sums[0] / entry_total
    down_scale = sums[1] / entry_total

    hidden = up_scale * hid_sum.astype(F32)
    inner = jnp.tanh(gelu_coef * (hidden + 0.044715 * hidden * hidden * hidden))
    act = (0.5 * hidden * (1.0 + inner)).astype(BF16)
    act_all = lax.all_gather(act, Z, axis=0, tiled=True)
    slope = 0.5 * (1.0 + inner) + 0.5 * hidden * (1.0 - inner * inner) * gelu_coef * (
        1.0 + 3.0 * 0.044715 * hidden * hidden
    )
    act_grad = down_scale * jnp.sum(act_parts.astype(F32), axis=0)
    hid_grad = (act_grad * slope).astype(BF16)
    copies = jnp.broadcast_to(hid_grad[None], (depth, *hid_grad.shape))
    hid_grad_all = lax.all_to_all(copies, Z, 0, 0, tiled=True).reshape(-1, hidden_width)

    ny, nx = lax.axis_size(Y), lax.axis_size(X)
    out_part = dot(act_all, down_tern, 1, 0).astype(BF16).reshape(ny, nx, half, 2 * width)
    out_rows = sent_home([out_part[:, d] for d in range(nx)], X).astype(BF16)
    out_sum = sent_home([out_rows[d] for d in range(ny)], Y)
    in_part = dot(hid_grad_all, up_tern, 1, 1).astype(BF16).reshape(ny, nx, half, 2 * width)
    in_rows = sent_home([in_part[d] for d in range(ny)], Y).astype(BF16)
    in_sum = sent_home([in_rows[d] for d in range(nx)], X)

    down_grad_theirs = (dot(act_all, grd_all[:, width:], 0, 0) * grad_norm).astype(BF16)
    up_grad_theirs = (dot(tok_all[:, width:], hid_grad_all, 0, 0) * grad_norm).astype(BF16)
    down_grad = (
        dot(act_all, grd_all[:, :width], 0, 0) * grad_norm + swapped(down_grad_theirs).astype(F32)
    ).astype(BF16)
    up_grad = (
        dot(tok_all[:, :width], hid_grad_all, 0, 0) * grad_norm
        + swapped(up_grad_theirs).astype(F32)
    ).astype(BF16)

    both = jnp.stack([down_scale * out_sum, up_scale * in_sum]).astype(BF16)
    own = both[:, :, :width]
    other = swapped(both[:, :, width:])
    both = jnp.where(
        core == 0,
        jnp.concatenate([own, other], axis=1),
        jnp.concatenate([other, own], axis=1),
    )
    return (both[0], both[1], up_grad, down_grad)


def solution(mesh):
    split = Mesh(mesh.devices.reshape(8, 2, 4, 4), (Z, C, Y, X))
    placed = (P(COL, ROW), P(ROW, COL), P(COL, ROW), P(COL, ROW))
    return jax.shard_map(
        body,
        mesh=split,
        in_specs=placed,
        out_specs=(P(COL, ROW), P(COL, ROW), P(ROW, COL), P(COL, ROW)),
        check_vma=False,
    )
```

```python
import math

import jax
import jax.numpy as jnp
from jax import lax
from jax.sharding import Mesh
from jax.sharding import PartitionSpec as P

Z, C, Y, X = "row_0", "row_1", "col_0", "col_1"
ROW = (Z, C)
COL = (Y, X)
F32 = jnp.float32
BF16 = jnp.bfloat16


gelu_coef = math.sqrt(2.0 / math.pi)


def shifted(value, axis, step):
    count = lax.axis_size(axis)
    return lax.ppermute(value, axis, [(i, (i + step) % count) for i in range(count)])


def swapped(value):
    return lax.ppermute(value, C, [(0, 1), (1, 0)])


def ternary(latent, fan_in):
    limit = 0.8 * fan_in ** (-0.5)
    wide = latent.astype(F32)
    return jnp.where(wide > limit, 1.0, jnp.where(wide < -limit, -1.0, 0.0)).astype(BF16)


def dot(left, right, left_dim, right_dim):
    return lax.dot_general(
        left, right, (((left_dim,), (right_dim,)), ((), ())), preferred_element_type=F32
    )


def ring_pieces(value, axis):
    count = lax.axis_size(axis)
    return [value] + [shifted(value, axis, -d) for d in range(1, count)]


def gathered(value, first, second):
    inner = jnp.stack(ring_pieces(value, first))
    return ring_pieces(inner, second)


def sent_home(pieces, axis):
    total = pieces[0].astype(F32)
    for d in range(1, len(pieces)):
        total = total + shifted(pieces[d], axis, d).astype(F32)
    return total


def total_of(latent):
    total = jnp.sum(jnp.abs(latent.astype(F32)))
    return jnp.broadcast_to(total, (8, 128))


def everyones(value, axes):
    count = lax.axis_size(axes)
    copies = jnp.broadcast_to(value[None], (count, *value.shape))
    return lax.all_to_all(copies, axes, 0, 0, tiled=True)


def body(tokens, up_latent, down_latent, out_grad):
    depth = lax.axis_size(Z)
    cols_axis = lax.axis_size(COL)
    rows_axis = lax.axis_size(ROW)
    core = lax.axis_index(C)
    fan_up = up_latent.shape[0] * rows_axis
    fan_down = down_latent.shape[0] * cols_axis
    entry_total = fan_up * fan_down
    width = tokens.shape[1]
    block = tokens.shape[0]
    half = block // 2
    token_total = block * cols_axis
    grad_norm = 1.0 / math.sqrt(token_total)

    pair = jnp.stack([tokens, out_grad])
    mine = lax.dynamic_slice_in_dim(pair, core * half, half, axis=1)
    theirs = lax.dynamic_slice_in_dim(pair, (1 - core) * half, half, axis=1)
    pair = jnp.concatenate([mine, swapped(theirs)], axis=2)
    up_other = swapped(up_latent)
    down_other = swapped(down_latent)

    tok = gathered(pair[0], X, Y)
    grd = gathered(pair[1], Y, X)
    tok_all = jnp.stack(tok, axis=0).reshape(-1, 2 * width)
    grd_all = jnp.stack(grd, axis=1).reshape(-1, 2 * width)

    up_tern = jnp.concatenate([ternary(up_latent, fan_up), ternary(up_other, fan_up)], axis=0)
    down_tern = jnp.concatenate(
        [ternary(down_latent, fan_down), ternary(down_other, fan_down)], axis=1
    )
    hidden_width = up_tern.shape[1]

    hid_part = dot(tok_all, up_tern, 1, 0).astype(BF16).reshape(depth, -1, hidden_width)
    hid_sum = lax.psum_scatter(hid_part, Z, scatter_dimension=0, tiled=False)
    act_part = dot(grd_all, down_tern, 1, 1).astype(BF16).reshape(depth, -1, hidden_width)
    act_sum = lax.psum_scatter(act_part, Z, scatter_dimension=0, tiled=False)

    sums = jnp.stack([total_of(up_latent), total_of(down_latent)])
    sums, _ = lax.optimization_barrier((sums, pair))
    for axes in (COL, ROW):
        sums = jnp.sum(everyones(sums, axes), axis=0)
    sums = sums[:, 0, 0]
    up_scale = sums[0] / entry_total
    down_scale = sums[1] / entry_total

    hidden = up_scale * hid_sum.astype(F32)
    inner = jnp.tanh(gelu_coef * (hidden + 0.044715 * hidden * hidden * hidden))
    act = (0.5 * hidden * (1.0 + inner)).astype(BF16)
    act_all = lax.all_gather(act, Z, axis=0, tiled=True)
    hid_sum, act_sum = lax.optimization_barrier((hid_sum, act_sum))
    hidden = up_scale * hid_sum.astype(F32)
    inner = jnp.tanh(gelu_coef * (hidden + 0.044715 * hidden * hidden * hidden))
    slope = 0.5 * (1.0 + inner) + 0.5 * hidden * (1.0 - inner * inner) * gelu_coef * (
        1.0 + 3.0 * 0.044715 * hidden * hidden
    )
    act_grad = down_scale * act_sum.astype(F32)
    hid_grad = (act_grad * slope).astype(BF16)
    hid_grad_all = lax.all_gather(hid_grad, Z, axis=0, tiled=True)

    ny, nx = lax.axis_size(Y), lax.axis_size(X)
    out_part = dot(act_all, down_tern, 1, 0).astype(BF16).reshape(ny, nx, half, 2 * width)
    out_rows = sent_home([out_part[:, d] for d in range(nx)], X).astype(BF16)
    out_sum = sent_home([out_rows[d] for d in range(ny)], Y)
    down_grad_theirs = (dot(act_all, grd_all[:, width:], 0, 0) * grad_norm).astype(BF16)
    down_grad = (
        dot(act_all, grd_all[:, :width], 0, 0) * grad_norm + swapped(down_grad_theirs).astype(F32)
    ).astype(BF16)

    hid_grad_all, out_sum, down_grad = lax.optimization_barrier((hid_grad_all, out_sum, down_grad))
    in_part = dot(hid_grad_all, up_tern, 1, 1).astype(BF16).reshape(ny, nx, half, 2 * width)
    in_rows = sent_home([in_part[d] for d in range(ny)], Y).astype(BF16)
    in_sum = sent_home([in_rows[d] for d in range(nx)], X)
    up_grad_theirs = (dot(tok_all[:, width:], hid_grad_all, 0, 0) * grad_norm).astype(BF16)
    up_grad = (
        dot(tok_all[:, :width], hid_grad_all, 0, 0) * grad_norm
        + swapped(up_grad_theirs).astype(F32)
    ).astype(BF16)

    both = jnp.stack([down_scale * out_sum, up_scale * in_sum]).astype(BF16)
    own = both[:, :, :width]
    other = swapped(both[:, :, width:])
    both = jnp.where(
        core == 0,
        jnp.concatenate([own, other], axis=1),
        jnp.concatenate([other, own], axis=1),
    )
    return (both[0], both[1], up_grad, down_grad)


def solution(mesh):
    split = Mesh(mesh.devices.reshape(8, 2, 4, 4), (Z, C, Y, X))
    placed = (P(COL, ROW), P(ROW, COL), P(COL, ROW), P(COL, ROW))
    return jax.shard_map(
        body,
        mesh=split,
        in_specs=placed,
        out_specs=(P(COL, ROW), P(COL, ROW), P(ROW, COL), P(COL, ROW)),
        check_vma=False,
    )
```

```python
import math

import jax
import jax.numpy as jnp
from jax import lax
from jax.sharding import Mesh
from jax.sharding import PartitionSpec as P


Z, C, Y, X = "row_0", "row_1", "col_0", "col_1"
ROW = (Z, C)
COL = (Y, X)
DEPTH = 8
F32 = jnp.float32
BF16 = jnp.bfloat16


gelu_coef = math.sqrt(2.0 / math.pi)


def shifted(value, axis, step):
    count = lax.axis_size(axis)
    return lax.ppermute(value, axis, [(i, (i + step) % count) for i in range(count)])


def swapped(value):
    return lax.ppermute(value, C, [(0, 1), (1, 0)])


def ternary(latent, fan_in):
    limit = 0.8 * fan_in ** (-0.5)
    wide = latent.astype(F32)
    return jnp.where(wide > limit, 1.0, jnp.where(wide < -limit, -1.0, 0.0)).astype(BF16)


def dot(left, right, left_dim, right_dim):
    return lax.dot_general(
        left, right, (((left_dim,), (right_dim,)), ((), ())), preferred_element_type=F32
    )


def ring_pieces(value, axis):
    pieces = [value]
    for d in range(1, lax.axis_size(axis)):
        pieces.append(shifted(value, axis, -d))
    return pieces


def sent_home(pieces, axis):
    total = pieces[0].astype(F32)
    for d in range(1, len(pieces)):
        moved = shifted(pieces[d], axis, d)
        total = total + moved.astype(F32)
    return total


def total_of(latent):
    return jnp.sum(jnp.abs(latent.astype(F32)))


WAYS = (1, -1, 1, -1)


def passed_on(value, stream):
    return shifted(value, Z, WAYS[stream])


def owner(index):
    return lax.bitwise_and(lax.axis_index(Z) + index % DEPTH, DEPTH - 1)


def block_of(index):
    which = owner(index)
    y_at = lax.shift_right_logical(which, 2)
    x_at = lax.bitwise_and(which, 3)
    return (4 * y_at + x_at, 2 * x_at + y_at)


def chunk(blocks, at):
    zero = jnp.zeros((), at.dtype)
    return lax.dynamic_slice(
        blocks, (at, zero, zero), (1, *blocks.shape[1:]), allow_negative_indices=False
    )[0]


def placed_at(full, value, at):
    zero = jnp.zeros((), at.dtype)
    return lax.dynamic_update_slice(
        full, value[None], (at, zero, zero), allow_negative_indices=False
    )


def split_rows(totals):
    kind = lax.broadcasted_iota(jnp.int32, totals.shape, 0) & 3
    high = lax.reduce_precision(totals, 8, 7)
    rest = totals - high
    middle = lax.reduce_precision(rest, 8, 7)
    low = rest - middle
    rows = jnp.where(kind == 0, high, jnp.where(kind == 1, middle, low))
    return jnp.where(kind == 3, 0.0, rows).astype(BF16)


def joined_rows(rows):
    lanes = rows.shape[-1]
    total = jnp.sum(rows.astype(F32).reshape(2, 4, lanes), axis=1, keepdims=True)
    return jnp.broadcast_to(total, (2, 4, lanes)).reshape(8, lanes)


def ring_sums(parts, totals):
    last = len(WAYS) - 1
    half = parts[0].shape[1]

    def own(i, index):
        return chunk(parts[i], block_of(index)[i // 2])

    moving = [own(i, -w) for i, w in enumerate(WAYS)]
    moving[last] = jnp.concatenate([moving[last], split_rows(totals)], axis=0)
    for s in range(DEPTH - 1):
        for i, way in enumerate(WAYS):
            came = passed_on(moving[i], i)
            total = came[:half].astype(F32) + own(i, -way * (s + 2)).astype(F32)
            if i == last:
                sums = joined_rows(came[half:]) + totals
            if s == DEPTH - 2:
                moving[i] = total
            elif i == last:
                moving[i] = jnp.concatenate([total.astype(BF16), split_rows(sums)], axis=0)
            else:
                moving[i] = total.astype(BF16)
    return moving, sums


def ring_all(values, spare):
    moving = list(values)
    full = [placed_at(f, v, block_of(0)[1 - i // 2]) for i, (f, v) in enumerate(zip(spare, values))]
    for s in range(DEPTH - 1):
        for i, way in enumerate(WAYS):
            moving[i] = passed_on(moving[i], i)
            full[i] = placed_at(full[i], moving[i], block_of(-way * (s + 1))[1 - i // 2])
    return full


def body(tokens, up_latent, down_latent, out_grad):
    cols_axis = lax.axis_size(COL)
    rows_axis = lax.axis_size(ROW)
    ny, nx = lax.axis_size(Y), lax.axis_size(X)
    core = lax.axis_index(C)
    fan_up = up_latent.shape[0] * rows_axis
    fan_down = down_latent.shape[0] * cols_axis
    entry_total = fan_up * fan_down
    width = tokens.shape[1]
    block = tokens.shape[0]
    half = block // 2
    token_total = block * cols_axis
    grad_norm = 1.0 / math.sqrt(token_total)

    pair = jnp.stack([tokens, out_grad])
    mine = lax.dynamic_slice_in_dim(pair, core * half, half, axis=1)
    theirs = lax.dynamic_slice_in_dim(pair, (1 - core) * half, half, axis=1)
    pair = jnp.concatenate([mine, swapped(theirs)], axis=2)

    at = lax.broadcasted_iota(jnp.int32, (8, 2 * width), 0)
    sums = jnp.where(at < 4, total_of(up_latent), total_of(down_latent))
    tok_near = jnp.stack(ring_pieces(pair[0], X))
    grd_near = jnp.concatenate([pair[1], split_rows(sums)], axis=0)
    grd_near = jnp.stack(ring_pieces(grd_near, Y))
    up_latent, down_latent, _, _ = lax.optimization_barrier(
        (up_latent, down_latent, tok_near, grd_near)
    )
    up_other = swapped(up_latent)
    down_other = swapped(down_latent)
    tok = jnp.stack(ring_pieces(tok_near, Y)).reshape(-1, 2 * width)
    grd = jnp.stack(ring_pieces(grd_near, X))
    sums = joined_rows(jnp.sum(grd[:, :, half:, :128].astype(F32), axis=(0, 1)))
    sums = sums + swapped(sums)
    grd = grd[:, :, :half].reshape(nx, 2, ny // 2, half, 2 * width)
    grd = jnp.moveaxis(grd, 1, 0).reshape(-1, 2 * width)

    up_tern = jnp.concatenate([ternary(up_latent, fan_up), ternary(up_other, fan_up)], axis=0)
    down_tern = jnp.concatenate(
        [ternary(down_latent, fan_down), ternary(down_other, fan_down)], axis=1
    )
    hidden_width = up_tern.shape[1]
    sums = jnp.broadcast_to(sums[:, :1], (8, hidden_width))

    hid_part = dot(tok, up_tern, 1, 0).astype(BF16).reshape(-1, half, hidden_width)
    hid_streams = lax.optimization_barrier(tuple(jnp.split(hid_part, 2)))
    act_part = dot(grd, down_tern, 1, 1).astype(BF16).reshape(-1, half, hidden_width)
    act_streams = lax.optimization_barrier(tuple(jnp.split(act_part, 2)))
    streams = [*hid_streams, *act_streams]
    totals, sums = ring_sums(streams, sums)
    up_scale = sums[0:1] / entry_total
    down_scale = sums[4:5] / entry_total

    acts, hid_grads = [], []
    for p in (0, 1):
        hidden = up_scale * totals[p]
        inner = jnp.tanh(gelu_coef * (hidden + 0.044715 * hidden * hidden * hidden))
        acts.append((0.5 * hidden * (1.0 + inner)).astype(BF16))
        slope = 0.5 * (1.0 + inner) + 0.5 * hidden * (1.0 - inner * inner) * gelu_coef * (
            1.0 + 3.0 * 0.044715 * hidden * hidden
        )
        hid_grads.append((down_scale * totals[2 + p] * slope).astype(BF16))
    full = ring_all([*acts, *hid_grads], streams)
    act, hid_grad = (
        [v.reshape(-1, hidden_width) for v in full[at : at + 2]] for at in (0, 2)
    )
    tok = jnp.split(tok, 2)
    grd = jnp.split(grd, 2)

    out_part = [
        dot(a, down_tern, 1, 0).astype(BF16).reshape(nx, ny // 2, half, 2 * width) for a in act
    ]
    out_rows = sent_home(
        [jnp.concatenate([o[d] for o in out_part], axis=0) for d in range(nx)], X
    ).astype(BF16)
    in_part = [
        dot(g, up_tern, 1, 1).astype(BF16).reshape(ny // 2, nx, half, 2 * width)
        for g in hid_grad
    ]
    in_rows = sent_home([i[d] for i in in_part for d in range(ny // 2)], Y).astype(BF16)

    def summed(lefts, rights):
        return sum(dot(l, r, 0, 0) for l, r in zip(lefts, rights)) * grad_norm

    down_other_grad = summed(act, [g[:, width:] for g in grd]).astype(BF16)
    up_other_grad = summed([t[:, width:] for t in tok], hid_grad).astype(BF16)
    down_grad = summed(act, [g[:, :width] for g in grd])
    down_grad = (down_grad + swapped(down_other_grad).astype(F32)).astype(BF16)
    up_grad = summed([t[:, :width] for t in tok], hid_grad)
    up_grad = (up_grad + swapped(up_other_grad).astype(F32)).astype(BF16)

    out_rows, down_grad, up_grad = lax.optimization_barrier((out_rows, down_grad, up_grad))
    out_sum = down_scale[:, : 2 * width] * sent_home([out_rows[d] for d in range(ny)], Y)
    in_sum = up_scale[:, : 2 * width] * sent_home([in_rows[d] for d in range(nx)], X)

    both = jnp.stack([out_sum, in_sum]).astype(BF16)
    own = both[:, :, :width]
    other = swapped(both[:, :, width:])
    both = jnp.where(
        core == 0,
        jnp.concatenate([own, other], axis=1),
        jnp.concatenate([other, own], axis=1),
    )
    return (both[0], both[1], up_grad, down_grad)


def solution(mesh):
    split = Mesh(mesh.devices.reshape(8, 2, 4, 4), (Z, C, Y, X))
    placed = (P(COL, ROW), P(ROW, COL), P(COL, ROW), P(COL, ROW))
    return jax.shard_map(
        body,
        mesh=split,
        in_specs=placed,
        out_specs=(P(COL, ROW), P(COL, ROW), P(ROW, COL), P(COL, ROW)),
        check_vma=False,
    )
```

```python
import math

import jax
import jax.numpy as jnp
from jax import lax
from jax.sharding import Mesh
from jax.sharding import PartitionSpec as P


Z, C, Y, X = "row_0", "row_1", "col_0", "col_1"
ROW = (Z, C)
COL = (Y, X)
DEPTH = 8
F32 = jnp.float32
BF16 = jnp.bfloat16


gelu_coef = math.sqrt(2.0 / math.pi)


def shifted(value, axis, step):
    count = lax.axis_size(axis)
    return lax.ppermute(value, axis, [(i, (i + step) % count) for i in range(count)])


def swapped(value):
    return lax.ppermute(value, C, [(0, 1), (1, 0)])


def ternary(latent, fan_in):
    limit = 0.8 * fan_in ** (-0.5)
    wide = latent.astype(F32)
    return jnp.where(wide > limit, 1.0, jnp.where(wide < -limit, -1.0, 0.0)).astype(BF16)


def dot(left, right, left_dim, right_dim):
    return lax.dot_general(
        left, right, (((left_dim,), (right_dim,)), ((), ())), preferred_element_type=F32
    )


def ring_pieces(value, axis):
    pieces = [value]
    for d in range(1, lax.axis_size(axis)):
        pieces.append(shifted(value, axis, -d))
    return pieces


def sent_home(pieces, axis):
    total = pieces[0].astype(F32)
    for d in range(1, len(pieces)):
        moved = shifted(pieces[d], axis, d)
        total = total + moved.astype(F32)
    return total


def total_of(latent):
    return jnp.sum(jnp.abs(latent.astype(F32)))


WAYS = (1, -1, 1, -1)


def passed_on(value, stream):
    return shifted(value, Z, WAYS[stream])


def owner(index):
    return lax.bitwise_and(lax.axis_index(Z) + index % DEPTH, DEPTH - 1)


def block_of(index):
    which = owner(index)
    y_at = lax.shift_right_logical(which, 2)
    x_at = lax.bitwise_and(which, 3)
    return (4 * y_at + x_at, 2 * x_at + y_at)


def chunk(blocks, at):
    zero = jnp.zeros((), at.dtype)
    return lax.dynamic_slice(
        blocks, (at, zero, zero), (1, *blocks.shape[1:]), allow_negative_indices=False
    )[0]


def placed_at(full, value, at):
    zero = jnp.zeros((), at.dtype)
    return lax.dynamic_update_slice(
        full, value[None], (at, zero, zero), allow_negative_indices=False
    )


def split_rows(totals):
    kind = lax.broadcasted_iota(jnp.int32, totals.shape, 0) & 3
    high = lax.reduce_precision(totals, 8, 7)
    rest = totals - high
    middle = lax.reduce_precision(rest, 8, 7)
    low = rest - middle
    rows = jnp.where(kind == 0, high, jnp.where(kind == 1, middle, low))
    return jnp.where(kind == 3, 0.0, rows).astype(BF16)


def joined_rows(rows):
    wide = rows.astype(F32)
    up = lax.broadcasted_iota(jnp.int32, wide.shape, 0) < 4
    up_total = jnp.sum(jnp.where(up, wide, 0.0), axis=0, keepdims=True)
    down_total = jnp.sum(jnp.where(up, 0.0, wide), axis=0, keepdims=True)
    return jnp.where(up, up_total, down_total)


def ring_sums(parts, totals):
    last = len(WAYS) - 1
    half = parts[0].shape[1]

    def own(i, index):
        return chunk(parts[i], block_of(index)[i // 2])

    moving = [own(i, -w) for i, w in enumerate(WAYS)]
    moving[last] = jnp.concatenate([moving[last], split_rows(totals)], axis=0)
    for s in range(DEPTH - 1):
        for i, way in enumerate(WAYS):
            came = passed_on(moving[i], i)
            total = came[:half].astype(F32) + own(i, -way * (s + 2)).astype(F32)
            if i == last:
                sums = joined_rows(came[half:]) + totals
            if s == DEPTH - 2:
                moving[i] = total
            elif i == last:
                moving[i] = jnp.concatenate([total.astype(BF16), split_rows(sums)], axis=0)
            else:
                moving[i] = total.astype(BF16)
    return moving, sums


def ring_all(values):
    moving = list(values)
    empty = jnp.zeros((DEPTH, *values[0].shape), BF16)
    full = [placed_at(empty, v, block_of(0)[1 - i // 2]) for i, v in enumerate(values)]
    for s in range(DEPTH - 1):
        for i, way in enumerate(WAYS):
            moving[i] = passed_on(moving[i], i)
            full[i] = placed_at(full[i], moving[i], block_of(-way * (s + 1))[1 - i // 2])
    return full


def body(tokens, up_latent, down_latent, out_grad):
    cols_axis = lax.axis_size(COL)
    rows_axis = lax.axis_size(ROW)
    ny, nx = lax.axis_size(Y), lax.axis_size(X)
    core = lax.axis_index(C)
    fan_up = up_latent.shape[0] * rows_axis
    fan_down = down_latent.shape[0] * cols_axis
    entry_total = fan_up * fan_down
    width = tokens.shape[1]
    block = tokens.shape[0]
    half = block // 2
    token_total = block * cols_axis
    grad_norm = 1.0 / math.sqrt(token_total)

    pair = jnp.stack([tokens, out_grad])
    mine = lax.dynamic_slice_in_dim(pair, core * half, half, axis=1)
    theirs = lax.dynamic_slice_in_dim(pair, (1 - core) * half, half, axis=1)
    pair = jnp.concatenate([mine, swapped(theirs)], axis=2)

    at = lax.broadcasted_iota(jnp.int32, (8, 2 * width), 0)
    sums = jnp.where(at < 4, total_of(up_latent), total_of(down_latent))
    tok_near = jnp.stack(ring_pieces(pair[0], X))
    grd_near = jnp.concatenate([pair[1], split_rows(sums)], axis=0)
    grd_near = jnp.stack(ring_pieces(grd_near, Y))
    up_latent, down_latent, _, _ = lax.optimization_barrier(
        (up_latent, down_latent, tok_near, grd_near)
    )
    up_other = swapped(up_latent)
    down_other = swapped(down_latent)
    tok = jnp.stack(ring_pieces(tok_near, Y)).reshape(-1, 2 * width)
    grd = jnp.stack(ring_pieces(grd_near, X))
    sums = joined_rows(jnp.sum(grd[:, :, half:, :128].astype(F32), axis=(0, 1)))
    sums = sums + swapped(sums)
    grd = grd[:, :, :half].reshape(nx, 2, ny // 2, half, 2 * width)
    grd = jnp.moveaxis(grd, 1, 0).reshape(-1, 2 * width)

    up_tern = jnp.concatenate([ternary(up_latent, fan_up), ternary(up_other, fan_up)], axis=0)
    down_tern = jnp.concatenate(
        [ternary(down_latent, fan_down), ternary(down_other, fan_down)], axis=1
    )
    hidden_width = up_tern.shape[1]
    sums = jnp.broadcast_to(sums[:, :1], (8, hidden_width))

    tok = jnp.split(tok, 2)
    grd = jnp.split(grd, 2)
    streams = [dot(t, up_tern, 1, 0) for t in tok]
    streams += [dot(g, down_tern, 1, 1) for g in grd]
    streams = [v.astype(BF16).reshape(DEPTH, half, hidden_width) for v in streams]
    totals, sums = ring_sums(streams, sums)
    up_scale = sums[0:1] / entry_total
    down_scale = sums[4:5] / entry_total

    acts, hid_grads = [], []
    for p in (0, 1):
        hidden = up_scale * totals[p]
        inner = jnp.tanh(gelu_coef * (hidden + 0.044715 * hidden * hidden * hidden))
        acts.append((0.5 * hidden * (1.0 + inner)).astype(BF16))
        slope = 0.5 * (1.0 + inner) + 0.5 * hidden * (1.0 - inner * inner) * gelu_coef * (
            1.0 + 3.0 * 0.044715 * hidden * hidden
        )
        hid_grads.append((down_scale * totals[2 + p] * slope).astype(BF16))
    full = ring_all([*acts, *hid_grads])
    act, hid_grad = (
        [v.reshape(-1, hidden_width) for v in full[at : at + 2]] for at in (0, 2)
    )

    out_part = [
        dot(a, down_tern, 1, 0).astype(BF16).reshape(nx, ny // 2, half, 2 * width) for a in act
    ]
    out_rows = sent_home(
        [jnp.concatenate([o[d] for o in out_part], axis=0) for d in range(nx)], X
    ).astype(BF16)
    in_part = [
        dot(g, up_tern, 1, 1).astype(BF16).reshape(ny // 2, nx, half, 2 * width)
        for g in hid_grad
    ]
    in_rows = sent_home([i[d] for i in in_part for d in range(ny // 2)], Y).astype(BF16)

    def summed(lefts, rights):
        return sum(dot(l, r, 0, 0) for l, r in zip(lefts, rights)) * grad_norm

    down_other_grad = summed(act, [g[:, width:] for g in grd]).astype(BF16)
    up_other_grad = summed([t[:, width:] for t in tok], hid_grad).astype(BF16)
    down_other_grad, up_other_grad = swapped(down_other_grad), swapped(up_other_grad)
    down_grad = summed(act, [g[:, :width] for g in grd])
    down_grad = (down_grad + down_other_grad.astype(F32)).astype(BF16)
    up_grad = summed([t[:, :width] for t in tok], hid_grad)
    up_grad = (up_grad + up_other_grad.astype(F32)).astype(BF16)

    out_sum = down_scale[:, : 2 * width] * sent_home([out_rows[d] for d in range(ny)], Y)
    in_sum = up_scale[:, : 2 * width] * sent_home([in_rows[d] for d in range(nx)], X)

    both = jnp.stack([out_sum, in_sum]).astype(BF16)
    own = both[:, :, :width]
    other = swapped(both[:, :, width:])
    both = jnp.where(
        core == 0,
        jnp.concatenate([own, other], axis=1),
        jnp.concatenate([other, own], axis=1),
    )
    return (both[0], both[1], up_grad, down_grad)


def solution(mesh):
    split = Mesh(mesh.devices.reshape(8, 2, 4, 4), (Z, C, Y, X))
    placed = (P(COL, ROW), P(ROW, COL), P(COL, ROW), P(COL, ROW))
    return jax.shard_map(
        body,
        mesh=split,
        in_specs=placed,
        out_specs=(P(COL, ROW), P(COL, ROW), P(ROW, COL), P(COL, ROW)),
        check_vma=False,
    )
```

```python
import math

import jax
import jax.numpy as jnp
from jax import lax
from jax.sharding import Mesh
from jax.sharding import PartitionSpec as P


Z, C, Y, X = "row_0", "row_1", "col_0", "col_1"
ROW = (Z, C)
COL = (Y, X)
DEPTH = 8
F32 = jnp.float32
BF16 = jnp.bfloat16


gelu_coef = math.sqrt(2.0 / math.pi)


def shifted(value, axis, step):
    count = lax.axis_size(axis)
    return lax.ppermute(value, axis, [(i, (i + step) % count) for i in range(count)])


def swapped(value):
    return lax.ppermute(value, C, [(0, 1), (1, 0)])


def ternary(latent, fan_in):
    limit = 0.8 * fan_in ** (-0.5)
    wide = latent.astype(F32)
    return jnp.where(wide > limit, 1.0, jnp.where(wide < -limit, -1.0, 0.0)).astype(BF16)


def dot(left, right, left_dim, right_dim):
    return lax.dot_general(
        left, right, (((left_dim,), (right_dim,)), ((), ())), preferred_element_type=F32
    )


def ring_pieces(value, axis):
    pieces = [value]
    for d in range(1, lax.axis_size(axis)):
        pieces.append(shifted(value, axis, -d))
    return pieces


def sent_home(pieces, axis):
    total = pieces[0].astype(F32)
    for d in range(1, len(pieces)):
        moved = shifted(pieces[d], axis, d)
        total = total + moved.astype(F32)
    return total


def total_of(latent):
    return jnp.sum(jnp.abs(latent.astype(F32)))


WAYS = (1, -1, 1, -1)


def passed_on(value, stream):
    return shifted(value, Z, WAYS[stream])


def owner(index):
    return lax.bitwise_and(lax.axis_index(Z) + index % DEPTH, DEPTH - 1)


def block_of(index):
    which = owner(index)
    y_at = lax.shift_right_logical(which, 2)
    x_at = lax.bitwise_and(which, 3)
    return (4 * y_at + x_at, 2 * x_at + y_at)


def chunk(blocks, at):
    zero = jnp.zeros((), at.dtype)
    return lax.dynamic_slice(
        blocks, (at, zero, zero), (1, *blocks.shape[1:]), allow_negative_indices=False
    )[0]


def placed_at(full, value, at):
    zero = jnp.zeros((), at.dtype)
    return lax.dynamic_update_slice(
        full, value[None], (at, zero, zero), allow_negative_indices=False
    )


def split_rows(totals):
    kind = lax.broadcasted_iota(jnp.int32, totals.shape, 0) & 3
    high = lax.reduce_precision(totals, 8, 7)
    rest = totals - high
    middle = lax.reduce_precision(rest, 8, 7)
    low = rest - middle
    rows = jnp.where(kind == 0, high, jnp.where(kind == 1, middle, low))
    return jnp.where(kind == 3, 0.0, rows).astype(BF16)


def joined_rows(rows):
    wide = rows.astype(F32)
    up = lax.broadcasted_iota(jnp.int32, wide.shape, 0) < 4
    up_total = jnp.sum(jnp.where(up, wide, 0.0), axis=0, keepdims=True)
    down_total = jnp.sum(jnp.where(up, 0.0, wide), axis=0, keepdims=True)
    return jnp.where(up, up_total, down_total)


def ring_sums(parts, totals):
    last = len(WAYS) - 1
    half = parts[0].shape[1]

    def own(i, index):
        return chunk(parts[i], block_of(index)[i // 2])

    moving = [own(i, -w) for i, w in enumerate(WAYS)]
    moving[last] = jnp.concatenate([moving[last], split_rows(totals)], axis=0)
    for s in range(DEPTH - 1):
        for i, way in enumerate(WAYS):
            came = passed_on(moving[i], i)
            total = came[:half].astype(F32) + own(i, -way * (s + 2)).astype(F32)
            if i == last:
                sums = joined_rows(came[half:]) + totals
            if i == last and s < DEPTH - 2:
                moving[i] = jnp.concatenate([total.astype(BF16), split_rows(sums)], axis=0)
            else:
                moving[i] = total.astype(BF16)
    return moving, sums


def ring_all(values):
    values = [lax.optimization_barrier(v) for v in values]
    moving = list(values)
    empty = jnp.zeros((DEPTH, *values[0].shape), BF16)
    full = [placed_at(empty, v, block_of(0)[1 - i // 2]) for i, v in enumerate(values)]
    for s in range(DEPTH - 1):
        for i, way in enumerate(WAYS):
            moving[i] = passed_on(moving[i], i)
            full[i] = placed_at(full[i], moving[i], block_of(-way * (s + 1))[1 - i // 2])
    return full


def body(tokens, up_latent, down_latent, out_grad):
    cols_axis = lax.axis_size(COL)
    rows_axis = lax.axis_size(ROW)
    ny, nx = lax.axis_size(Y), lax.axis_size(X)
    core = lax.axis_index(C)
    fan_up = up_latent.shape[0] * rows_axis
    fan_down = down_latent.shape[0] * cols_axis
    entry_total = fan_up * fan_down
    width = tokens.shape[1]
    block = tokens.shape[0]
    half = block // 2
    token_total = block * cols_axis
    grad_norm = 1.0 / math.sqrt(token_total)

    pair = jnp.stack([tokens, out_grad])
    mine = lax.dynamic_slice_in_dim(pair, core * half, half, axis=1)
    theirs = lax.dynamic_slice_in_dim(pair, (1 - core) * half, half, axis=1)
    pair = jnp.concatenate([mine, swapped(theirs)], axis=2)

    at = lax.broadcasted_iota(jnp.int32, (8, 2 * width), 0)
    sums = jnp.where(at < 4, total_of(up_latent), total_of(down_latent))
    tok_near = jnp.stack(ring_pieces(pair[0], X))
    grd_near = jnp.concatenate([pair[1], split_rows(sums)], axis=0)
    grd_near = jnp.stack(ring_pieces(grd_near, Y))
    up_latent, down_latent, _, _ = lax.optimization_barrier(
        (up_latent, down_latent, tok_near, grd_near)
    )
    up_other = swapped(up_latent)
    down_other = swapped(down_latent)
    tok = jnp.stack(ring_pieces(tok_near, Y)).reshape(-1, 2 * width)
    grd = jnp.stack(ring_pieces(grd_near, X))
    sums = joined_rows(jnp.sum(grd[:, :, half:, :128].astype(F32), axis=(0, 1)))
    sums = sums + swapped(sums)
    grd = grd[:, :, :half].reshape(nx, 2, ny // 2, half, 2 * width)
    grd = jnp.moveaxis(grd, 1, 0).reshape(-1, 2 * width)

    up_tern = jnp.concatenate([ternary(up_latent, fan_up), ternary(up_other, fan_up)], axis=0)
    down_tern = jnp.concatenate(
        [ternary(down_latent, fan_down), ternary(down_other, fan_down)], axis=1
    )
    hidden_width = up_tern.shape[1]
    sums = jnp.broadcast_to(sums[:, :1], (8, hidden_width))

    tok = jnp.split(tok, 2)
    grd = jnp.split(grd, 2)
    streams = [dot(t, up_tern, 1, 0) for t in tok]
    streams += [dot(g, down_tern, 1, 1) for g in grd]
    streams = [v.astype(BF16).reshape(DEPTH, half, hidden_width) for v in streams]
    streams = lax.optimization_barrier(streams)
    totals, sums = ring_sums(streams, sums)
    up_scale = sums[0:1] / entry_total
    down_scale = sums[4:5] / entry_total

    acts, hid_grads = [], []
    for p in (0, 1):
        hidden = up_scale * totals[p]
        inner = jnp.tanh(gelu_coef * (hidden + 0.044715 * hidden * hidden * hidden))
        acts.append((0.5 * hidden * (1.0 + inner)).astype(BF16))
        slope = 0.5 * (1.0 + inner) + 0.5 * hidden * (1.0 - inner * inner) * gelu_coef * (
            1.0 + 3.0 * 0.044715 * hidden * hidden
        )
        hid_grads.append((down_scale * totals[2 + p] * slope).astype(BF16))
    full = ring_all([*acts, *hid_grads])
    act, hid_grad = (
        [v.reshape(-1, hidden_width) for v in full[at : at + 2]] for at in (0, 2)
    )

    out_part = [
        dot(a, down_tern, 1, 0).astype(BF16).reshape(nx, ny // 2, half, 2 * width) for a in act
    ]
    out_rows = sent_home(
        [jnp.concatenate([o[d] for o in out_part], axis=0) for d in range(nx)], X
    ).astype(BF16)
    in_part = [
        dot(g, up_tern, 1, 1).astype(BF16).reshape(ny // 2, nx, half, 2 * width)
        for g in hid_grad
    ]
    in_rows = sent_home([i[d] for i in in_part for d in range(ny // 2)], Y).astype(BF16)

    def summed(lefts, rights):
        return sum(dot(l, r, 0, 0) for l, r in zip(lefts, rights)) * grad_norm

    down_other_grad = summed(act, [g[:, width:] for g in grd]).astype(BF16)
    up_other_grad = summed([t[:, width:] for t in tok], hid_grad).astype(BF16)
    down_other_grad, up_other_grad = swapped(down_other_grad), swapped(up_other_grad)
    down_grad = summed(act, [g[:, :width] for g in grd])
    down_grad = (down_grad + down_other_grad.astype(F32)).astype(BF16)
    up_grad = summed([t[:, :width] for t in tok], hid_grad)
    up_grad = (up_grad + up_other_grad.astype(F32)).astype(BF16)

    out_sum = down_scale[:, : 2 * width] * sent_home([out_rows[d] for d in range(ny)], Y)
    in_sum = up_scale[:, : 2 * width] * sent_home([in_rows[d] for d in range(nx)], X)

    both = jnp.stack([out_sum, in_sum]).astype(BF16)
    own = both[:, :, :width]
    other = swapped(both[:, :, width:])
    both = jnp.where(
        core == 0,
        jnp.concatenate([own, other], axis=1),
        jnp.concatenate([other, own], axis=1),
    )
    return (both[0], both[1], up_grad, down_grad)


def solution(mesh):
    split = Mesh(mesh.devices.reshape(8, 2, 4, 4), (Z, C, Y, X))
    placed = (P(COL, ROW), P(ROW, COL), P(COL, ROW), P(COL, ROW))
    return jax.shard_map(
        body,
        mesh=split,
        in_specs=placed,
        out_specs=(P(COL, ROW), P(COL, ROW), P(ROW, COL), P(COL, ROW)),
        check_vma=False,
    )
```
